512 devices in a mesh: rows: 64 (over x, z, core), cols: 8 (over y).
Axes of the slice: x: 4, y: 8, z: 8, core: 2. Of those that a mesh axis runs over, the one named last changes fastest.
Arguments:
- sample_embeddings: bfloat16 [131072, 256], P(('rows', 'cols')), may hold values from -0.5 to 0.5
- reference_embeddings: bfloat16 [8192, 256], P(('cols', 'rows')), may hold values from -0.5 to 0.5
- sample_mass: float32 [131072], P('rows'), may hold values from 0.05 to 20
- reference_mass: float32 [8192], P('cols'), may hold values from 0.05 to 20
- start_potential: float32 [8192], P('cols'), may hold values from -1.5 to 31.7
- tile_pairs: int32 [64, 8, 2, 48], P('rows', 'cols'), may hold values from 0 to 15, as said below
- tile_counts: int32 [64, 8], P('rows', 'cols'), may hold values from 16 to 48, as said below
Outputs:
- sample_potential: float32 [131072], P('rows')
- reference_potential: float32 [8192], P('cols')
The draws below stay inside these ranges and needn't reach their ends.
Inputs may be any that keep to these rules, and one draw needn't show every extreme that they name: tile_pairs[a, b, 0, t] is a row tile (below 16) and tile_pairs[a, b, 1, t] a column tile (below 8) of device (a, b); only the first tile_counts[a, b] slots are in use, the rest hold other valid pairs; used pairs of a device are distinct, and every row tile and every column tile of a device appears among its used pairs. `tile_counts`: some device uses all 48 slots in every draw.
All inputs are finite; a program needn't handle non-finite values.
Results may differ from the reference program's by a relative error of at most 0.0003.
Values may be sent and summed in bfloat16 or wider, within the bound.
A program may use at most 64 MiB of HBM per device.

```python
import math
import jax
import jax.numpy as jnp
from jax import lax

E = 256
TILE = 128
R_DEV = 2048
C_DEV = 1024
ITERS = 2
RT = 16
CT = 8
MAXT = 48
SAMPLES = 131072
REFERENCES = 8192
N_ROWS = 64
N_COLS = 8


def tile_plan(key):
    devices = N_ROWS * N_COLS
    pairs_total = RT * CT
    in_use = jax.random.randint(jax.random.fold_in(key, 11), (devices,), RT, MAXT + 1)
    busiest = jax.random.randint(jax.random.fold_in(key, 12), (), 0, devices)
    in_use = in_use.at[busiest].set(MAXT)
    shifts = jax.random.randint(jax.random.fold_in(key, 13), (devices,), 0, CT)
    first_keys = jax.random.split(jax.random.fold_in(key, 14), devices)
    second_keys = jax.random.split(jax.random.fold_in(key, 15), devices)

    def one_device(shift_value, in_use_value, first_key, second_key):
        pair_ids = jnp.arange(pairs_total, dtype=jnp.int32)
        row_ids = pair_ids // CT
        column_ids = pair_ids % CT
        covering = column_ids == (row_ids + shift_value) % CT
        first_rank = jax.random.permutation(first_key, pairs_total).astype(jnp.int32)
        priority = jnp.where(covering, first_rank - pairs_total, first_rank)
        placing = jnp.argsort(priority)
        standing = jnp.argsort(placing)
        chosen = standing < in_use_value
        second_rank = jax.random.permutation(second_key, pairs_total).astype(jnp.int32)
        ordering = jnp.argsort(jnp.where(chosen, second_rank, second_rank + pairs_total))[:MAXT]
        return jnp.stack([ordering // CT, ordering % CT]).astype(jnp.int32)
    layout = jax.vmap(one_device)(shifts, in_use, first_keys, second_keys)
    return (layout.reshape(N_ROWS, N_COLS, 2, MAXT), in_use.reshape(N_ROWS, N_COLS).astype(jnp.int32))


def draw_tile_pairs(key, part):
    return tile_plan(key)[0]


def draw_tile_counts(key, part):
    return tile_plan(key)[1]


def draw_start_potential(key, part):
    base = jnp.clip(0.3 * jax.random.normal(jax.random.fold_in(key, 21), (REFERENCES,), jnp.float32), -1.5, 1.5)
    return base.astype(jnp.float32)


def level_of(own_key, shape, cuts, smallest, top_value):
    def one(position, parts):
        draws = jax.random.uniform(jax.random.fold_in(jax.random.fold_in(own_key, 6), position), (parts,), jnp.float32, smallest / len(cuts), top_value / len(cuts))
        return jnp.repeat(jnp.exp(draws), shape[position] // parts).reshape((-1,) + (1,) * (len(shape) - position - 1))

    gain = one(*cuts[0])
    for cut in cuts[1:]:
        gain = gain * one(*cut)
    return gain


def normal_values(rng, extent, width, reach, pieces=(), kind=jnp.bfloat16):
    result = width * jax.random.normal(rng, extent, jnp.float32)
    if pieces:
        result = result * level_of(rng, extent, pieces, -0.22, 0.18)
    return jnp.clip(result, -reach, reach).astype(kind)


def setup_inputs(seed: int = 0) -> dict:
    streams_of = jax.random.split(jax.random.key(seed), 8)
    return {
        "sample_embeddings": normal_values(streams_of[0], (SAMPLES, E), 0.0625, 0.5, ((0, 512),)),
        "reference_embeddings": normal_values(streams_of[1], (REFERENCES, E), 0.0625, 0.5, ((0, 512),)),
        "sample_mass": jnp.clip(jnp.exp(math.log(20.0) - 5.9914645 * jax.random.uniform(streams_of[2], (SAMPLES,), jnp.float32) ** level_of(streams_of[2], (SAMPLES,), ((0, 64),), -0.2, 0.2)), 0.05, 20.0),
        "reference_mass": jnp.clip(jnp.exp(math.log(20.0) - 5.9914645 * jax.random.uniform(streams_of[3], (REFERENCES,), jnp.float32) ** level_of(streams_of[3], (REFERENCES,), ((0, 8),), -0.2, 0.2)), 0.05, 20.0),
        "start_potential": draw_start_potential(jax.random.fold_in(streams_of[7], 71), 0),
        "tile_pairs": draw_tile_pairs(jax.random.fold_in(streams_of[7], 71), 0),
        "tile_counts": draw_tile_counts(jax.random.fold_in(streams_of[7], 71), 0),
    }


entropy = 0.1
lowest = -1e30


def device_costs(row_block, column_block, row_ids, column_ids):
    row_tiles = row_block.reshape(RT, TILE, E)[row_ids].astype(jnp.float32)
    column_tiles = column_block.reshape(CT, TILE, E)[column_ids].astype(jnp.float32)
    inner = jnp.einsum("tie,tje->tij", row_tiles, column_tiles, precision=lax.Precision.HIGHEST)
    row_sq = jnp.sum(row_tiles * row_tiles, axis=2)
    column_sq = jnp.sum(column_tiles * column_tiles, axis=2)
    return row_sq[:, :, None] + column_sq[:, None, :] - 2.0 * inner


def device_pass(device, sample_embeddings, reference_embeddings, potential, tile_pairs, tile_counts, along_rows):
    row_group = device // N_COLS
    column_group = device % N_COLS
    row_block = lax.dynamic_slice_in_dim(sample_embeddings, (row_group * R_DEV).astype(jnp.int32), R_DEV, 0)
    column_block = lax.dynamic_slice_in_dim(reference_embeddings, (column_group * C_DEV).astype(jnp.int32), C_DEV, 0)
    pairs = tile_pairs.reshape(N_ROWS * N_COLS, 2, MAXT)[device]
    usable = jnp.arange(MAXT, dtype=jnp.int32) < tile_counts.reshape(-1)[device]
    costs = device_costs(row_block, column_block, pairs[0], pairs[1])
    if along_rows:
        part = lax.dynamic_slice_in_dim(potential, (column_group * C_DEV).astype(jnp.int32), C_DEV, 0).reshape(CT, TILE)
        scores = (part[pairs[1]][:, None, :] - costs) / entropy
        tile_peak = jnp.where(usable[:, None], jnp.max(scores, axis=2), lowest)
        peak = jnp.full((RT, TILE), lowest, jnp.float32).at[pairs[0]].max(tile_peak)
        exp_sums = jnp.sum(jnp.exp(scores - peak[pairs[0]][:, :, None]), axis=2)
        exp_sums = jnp.where(usable[:, None], exp_sums, 0.0)
        total = jnp.zeros((RT, TILE), jnp.float32).at[pairs[0]].add(exp_sums)
    else:
        part = lax.dynamic_slice_in_dim(potential, (row_group * R_DEV).astype(jnp.int32), R_DEV, 0).reshape(RT, TILE)
        scores = (part[pairs[0]][:, :, None] - costs) / entropy
        tile_peak = jnp.where(usable[:, None], jnp.max(scores, axis=1), lowest)
        peak = jnp.full((CT, TILE), lowest, jnp.float32).at[pairs[1]].max(tile_peak)
        exp_sums = jnp.sum(jnp.exp(scores - peak[pairs[1]][:, None, :]), axis=1)
        exp_sums = jnp.where(usable[:, None], exp_sums, 0.0)
        total = jnp.zeros((CT, TILE), jnp.float32).at[pairs[1]].add(exp_sums)
    return peak, total


def reference(sample_embeddings, reference_embeddings, sample_mass, reference_mass, start_potential, tile_pairs, tile_counts):
    devices = jnp.arange(N_ROWS * N_COLS, dtype=jnp.int32)
    reference_potential = start_potential
    sample_potential = jnp.zeros_like(sample_mass)
    for iteration in range(ITERS):
        def row_device(device):
            return device_pass(device, sample_embeddings, reference_embeddings, reference_potential, tile_pairs, tile_counts, True)

        peak, total = lax.map(row_device, devices)
        peak = peak.reshape(N_ROWS, N_COLS, R_DEV)
        total = total.reshape(N_ROWS, N_COLS, R_DEV)
        larger = jnp.max(peak, axis=1)
        summed = jnp.sum(total * jnp.exp(peak - larger[:, None, :]), axis=1)
        sample_potential = entropy * jnp.log(sample_mass) - entropy * (larger + jnp.log(summed)).reshape(-1)

        def column_device(device):
            return device_pass(device, sample_embeddings, reference_embeddings, sample_potential, tile_pairs, tile_counts, False)

        peak, total = lax.map(column_device, devices)
        peak = peak.reshape(N_ROWS, N_COLS, C_DEV)
        total = total.reshape(N_ROWS, N_COLS, C_DEV)
        larger = jnp.max(peak, axis=0)
        summed = jnp.sum(total * jnp.exp(peak - larger[None, :, :]), axis=0)
        reference_potential = entropy * jnp.log(reference_mass) - entropy * (larger + jnp.log(summed)).reshape(-1)
    return sample_potential, reference_potential
```

```python
import math

import jax
import jax.numpy as jnp
from jax import lax
from jax.experimental import pallas as pl
from jax.experimental.pallas import tpu as pltpu
from jax.sharding import PartitionSpec as P

TILE = 128
ITERS = 2
WIDTH = 256
ROW_TILES = 16
COLUMN_TILES = 8
SLOTS = 48
PIECES = 4
FAR_FIRST = (4, 3, 5, 2, 6, 1, 7)

SCALE = math.log2(math.e) / 0.1
LOWEST = -1e30
MESH = pl.DeviceIdType.MESH


def remote(source, target, send_sem, recv_sem, device):
    return pltpu.make_async_remote_copy(
        src_ref=source,
        dst_ref=target,
        send_sem=send_sem,
        recv_sem=recv_sem,
        device_id=device,
        device_id_type=MESH,
    )


def tile_norms(load_tile, count):
    padded = max(count, 16)
    ones = jnp.ones((padded, WIDTH), jnp.bfloat16)
    place = lax.broadcasted_iota(jnp.int32, (padded, TILE), 0)

    def one(tile, found):
        values = load_tile(tile).astype(jnp.float32)
        squares = values * values
        high = squares.astype(jnp.bfloat16)
        low = (squares - high.astype(jnp.float32)).astype(jnp.bfloat16)
        sums = dot_rows(ones, high) + dot_rows(ones, low)
        return jnp.where(place == tile, sums, found)

    found = lax.fori_loop(0, count, one, jnp.zeros((padded, TILE), jnp.float32))
    return found[:count]


def dot_rows(left, right):
    return lax.dot_general(
        left, right, (((1,), (1,)), ((), ())), preferred_element_type=jnp.float32
    )


def spread(values, spread_ref):
    turned = values.T
    for tile in range(values.shape[0]):
        spread_ref[tile] = jnp.broadcast_to(turned[:, tile : tile + 1], (TILE, TILE))


def log_sum(parts):
    peak = jnp.max(parts, axis=0)
    return peak + jnp.log2(jnp.sum(jnp.exp2(parts - peak[None]), axis=0))


def kernel(
    samples,
    references,
    sample_mass,
    reference_mass,
    start,
    pairs,
    counts,
    sample_out,
    reference_out,
    row_buf,
    column_buf,
    column_major,
    row_major,
    column_spread,
    row_spread,
    slot_peak,
    slot_total,
    row_bias,
    column_bias,
    y_buf,
    x_buf,
    z_buf,
    own_sem,
    ring_send,
    ring_recv,
    gather_send,
    gather_recv,
    y_send,
    y_recv,
    x_send,
    x_recv,
    z_send,
    z_recv,
):
    row = lax.axis_index("rows")
    y = lax.axis_index("cols")
    x = lax.div(row, 16)
    z = lax.rem(lax.div(row, 2), 8)
    core = lax.rem(row, 2)
    corner = x * 2 + core

    def at(px, pz, pcore):
        return ((px * 8 + pz) * 2 + pcore, y)

    def y_peer(step):
        return (row, lax.rem(y + step, 8))

    def z_peer(step):
        return at(x, lax.rem(z + step, 8), core)

    def corner_peer(step):
        other = lax.rem(corner + step, 8)
        return at(lax.div(other, 2), z, lax.rem(other, 2))

    barrier = pltpu.get_barrier_semaphore()
    for step in FAR_FIRST:
        for peer in (y_peer(step), z_peer(step), corner_peer(step)):
            pl.semaphore_signal(barrier, inc=1, device_id=peer, device_id_type=MESH)

    def block_of(px, pz, pcore):
        return column_buf.at[px * 2 + lax.div(pz, 4), lax.rem(pz, 4), pcore]

    own_copies = [
        pltpu.make_async_copy(
            samples.at[pl.ds(64 * piece, 64)],
            row_buf.at[2 * y + piece // 2, piece % 2],
            own_sem.at[piece],
        )
        for piece in range(PIECES)
    ]
    own_copies.append(
        pltpu.make_async_copy(references, block_of(x, z, core), own_sem.at[PIECES])
    )
    for copy in own_copies:
        copy.start()

    in_use = counts[0, 0]
    row_place = lax.broadcasted_iota(jnp.int32, (ROW_TILES, TILE), 0)
    column_place = lax.broadcasted_iota(jnp.int32, (COLUMN_TILES, TILE), 0)

    def mark(slot, carry):
        spare = jnp.where(slot < in_use, 0.0, LOWEST).astype(jnp.float32)
        row_bias[slot] = jnp.where(row_place == pairs[0, 0, 0, slot], spare, LOWEST)
        column_bias[slot] = jnp.where(column_place == pairs[0, 0, 1, slot], spare, LOWEST)
        return carry

    lax.fori_loop(0, SLOTS, mark, 0)

    pl.semaphore_wait(barrier, 21)

    z_copies = []
    for step in FAR_FIRST:
        copy = remote(
            references,
            block_of(x, z, core),
            gather_send.at[step],
            gather_recv.at[step],
            z_peer(step),
        )
        copy.start()
        z_copies.append(copy)

    ring = {}

    def ring_start(hop, piece):
        for side in (0, 1):
            if hop == 4 and (piece < 2) != (side == 0):
                continue
            back = hop - 1
            block = lax.rem(y + (8 - back if side == 0 else back), 8)
            landing = row_buf.at[2 * block + piece // 2, piece % 2]
            source = samples.at[pl.ds(64 * piece, 64)] if hop == 1 else landing
            copy = remote(
                source,
                landing,
                ring_send.at[side, hop - 1, piece],
                ring_recv.at[side, hop - 1, piece],
                y_peer(1 if side == 0 else 7),
            )
            copy.start()
            ring[side, hop, piece] = copy

    def ring_wait(hop, piece):
        for side in (0, 1):
            if (side, hop, piece) in ring:
                ring[side, hop, piece].wait_recv()

    for piece in range(PIECES):
        ring_start(1, piece)
    for piece in range(PIECES):
        ring_wait(1, piece)
        ring_start(2, piece)

    for copy in own_copies:
        copy.wait()
    for copy in z_copies:
        copy.wait_recv()
    x_copies = []
    for step in (2, 1, 3):
        mine = column_buf.at[pl.ds(2 * x, 2), :, core]
        copy = remote(
            mine,
            mine,
            gather_send.at[7 + step],
            gather_recv.at[7 + step],
            at(lax.rem(x + step, 4), z, core),
        )
        copy.start()
        x_copies.append(copy)

    for piece in range(PIECES):
        ring_wait(2, piece)
        ring_start(3, piece)
    for piece in range(PIECES):
        ring_wait(3, piece)
        ring_start(4, piece)

    for copy in x_copies:
        copy.wait_recv()
    mine = column_buf.at[:, :, core]
    core_copy = remote(
        mine, mine, gather_send.at[11], gather_recv.at[11], at(x, z, 1 - core)
    )
    core_copy.start()
    core_copy.wait_recv()

    def row_tile(tile):
        return row_buf[tile].reshape(TILE, WIDTH)

    def column_tile(tile):
        return column_buf[tile].reshape(TILE, WIDTH)

    column_norms = tile_norms(column_tile, COLUMN_TILES)
    spread(SCALE * (start[...] - column_norms), column_spread)

    for piece in range(PIECES):
        ring_wait(4, piece)

    def multiply(slot, carry):
        row_values = row_tile(pairs[0, 0, 0, slot])
        column_values = column_tile(pairs[0, 0, 1, slot])
        column_major[slot] = (2.0 * SCALE) * dot_rows(column_values, row_values)
        row_major[slot] = (2.0 * SCALE) * dot_rows(row_values, column_values)
        return carry

    lax.fori_loop(0, SLOTS, multiply, 0, unroll=2)

    def local_pass(products, spread_ref, axis, bias):
        def one(slot, carry):
            scores = products[slot] + spread_ref[pairs[0, 0, axis, slot]]
            peak = jnp.max(scores, axis=0, keepdims=True)
            slot_peak[pl.ds(slot, 1), :] = peak
            slot_total[pl.ds(slot, 1), :] = jnp.sum(
                jnp.exp2(scores - peak), axis=0, keepdims=True
            )
            return carry

        lax.fori_loop(0, SLOTS, one, 0, unroll=4)
        slot_peak[...] = slot_peak[...] + jnp.log2(slot_total[...])

        shape = bias.shape[1:]

        def highest(slot, peak):
            return jnp.maximum(peak, slot_peak[pl.ds(slot, 1), :] + bias[slot])

        peak = lax.fori_loop(
            0, SLOTS, highest, jnp.full(shape, LOWEST, jnp.float32), unroll=8
        )

        def collect(slot, total):
            return total + jnp.exp2(slot_peak[pl.ds(slot, 1), :] + bias[slot] - peak)

        total = lax.fori_loop(
            0, SLOTS, collect, jnp.zeros(shape, jnp.float32), unroll=8
        )
        return peak + jnp.log2(total)

    def exchange(value, buf, iteration, place, peer, send_sem, recv_sem):
        buf[iteration, place] = value
        copies = []
        for step in FAR_FIRST:
            mine = buf.at[iteration, place]
            copy = remote(
                mine,
                mine,
                send_sem.at[iteration, step],
                recv_sem.at[iteration, step],
                peer(step),
            )
            copy.start()
            copies.append(copy)
        return copies

    def finish(copies, buf, iteration):
        for copy in copies:
            copy.wait()
        return log_sum(buf[iteration])

    sample_logs = jnp.log2(sample_mass[...])
    reference_logs = jnp.log2(reference_mass[...])
    for iteration in range(ITERS):
        value = local_pass(column_major, column_spread, 1, row_bias)
        copies = exchange(value, y_buf, iteration, y, y_peer, y_send, y_recv)
        if iteration == 0:
            row_norms = tile_norms(row_tile, ROW_TILES)
        row_level = sample_logs - finish(copies, y_buf, iteration)
        spread(row_level, row_spread)
        if iteration == ITERS - 1:
            sample_out[...] = row_level * (1.0 / SCALE) + row_norms
        value = local_pass(row_major, row_spread, 0, column_bias)
        copies = exchange(value, x_buf, iteration, corner, corner_peer, x_send, x_recv)
        value = finish(copies, x_buf, iteration)
        copies = exchange(value, z_buf, iteration, z, z_peer, z_send, z_recv)
        column_level = reference_logs - finish(copies, z_buf, iteration)
        if iteration < ITERS - 1:
            spread(column_level, column_spread)
        else:
            reference_out[...] = column_level * (1.0 / SCALE) + column_norms

    for copy in ring.values():
        copy.wait_send()
    for copy in z_copies + x_copies + [core_copy]:
        copy.wait_send()


def body(
    sample_embeddings,
    reference_embeddings,
    sample_mass,
    reference_mass,
    start_potential,
    tile_pairs,
    tile_counts,
):
    vmem = pl.BlockSpec(memory_space=pltpu.VMEM)
    smem = pl.BlockSpec(memory_space=pltpu.SMEM)
    anywhere = pl.BlockSpec(memory_space=pl.ANY)
    dma = pltpu.SemaphoreType.DMA
    sample_out, reference_out = pl.pallas_call(
        kernel,
        out_shape=(
            jax.ShapeDtypeStruct((ROW_TILES, TILE), jnp.float32),
            jax.ShapeDtypeStruct((COLUMN_TILES, TILE), jnp.float32),
        ),
        in_specs=[anywhere, anywhere, vmem, vmem, vmem, smem, smem],
        out_specs=(vmem, vmem),
        scratch_shapes=[
            pltpu.VMEM((ROW_TILES, 2, 64, WIDTH), jnp.bfloat16),
            pltpu.VMEM((COLUMN_TILES, 4, 2, 16, WIDTH), jnp.bfloat16),
            pltpu.VMEM((SLOTS, TILE, TILE), jnp.float32),
            pltpu.VMEM((SLOTS, TILE, TILE), jnp.float32),
            pltpu.VMEM((COLUMN_TILES, TILE, TILE), jnp.float32),
            pltpu.VMEM((ROW_TILES, TILE, TILE), jnp.float32),
            pltpu.VMEM((SLOTS, TILE), jnp.float32),
            pltpu.VMEM((SLOTS, TILE), jnp.float32),
            pltpu.VMEM((SLOTS, ROW_TILES, TILE), jnp.float32),
            pltpu.VMEM((SLOTS, COLUMN_TILES, TILE), jnp.float32),
            pltpu.VMEM((ITERS, 8, ROW_TILES, TILE), jnp.float32),
            pltpu.VMEM((ITERS, 8, COLUMN_TILES, TILE), jnp.float32),
            pltpu.VMEM((ITERS, 8, COLUMN_TILES, TILE), jnp.float32),
            dma((PIECES + 1,)),
            dma((2, 4, PIECES)),
            dma((2, 4, PIECES)),
            dma((12,)),
            dma((12,)),
            dma((ITERS, 8)),
            dma((ITERS, 8)),
            dma((ITERS, 8)),
            dma((ITERS, 8)),
            dma((ITERS, 8)),
            dma((ITERS, 8)),
        ],
        compiler_params=pltpu.CompilerParams(collective_id=0, has_side_effects=True),
    )(
        sample_embeddings,
        reference_embeddings,
        sample_mass.reshape(ROW_TILES, TILE),
        reference_mass.reshape(COLUMN_TILES, TILE),
        start_potential.reshape(COLUMN_TILES, TILE),
        tile_pairs,
        tile_counts,
    )
    return (sample_out.reshape(-1), reference_out.reshape(-1))


def solution(mesh):
    placed = (
        P(("rows", "cols"), None),
        P(("cols", "rows"), None),
        P("rows"),
        P("cols"),
        P("cols"),
        P("rows", "cols", None, None),
        P("rows", "cols"),
    )
    return jax.shard_map(
        body, mesh=mesh, in_specs=placed, out_specs=(P("rows"), P("cols")), check_vma=False
    )
```

```python
import math

import jax
import jax.numpy as jnp
from jax import lax
from jax.experimental import pallas as pl
from jax.experimental.pallas import tpu as pltpu
from jax.sharding import PartitionSpec as P

TILE = 128
ITERS = 2
WIDTH = 256
ROW_TILES = 16
COLUMN_TILES = 8
SLOTS = 48
PIECES = 4
FAR_FIRST = (4, 3, 5, 2, 6, 1, 7)

SCALE = math.log2(math.e) / 0.1
LOWEST = -1e30
MESH = pl.DeviceIdType.MESH


def remote(source, target, send_sem, recv_sem, device):
    return pltpu.make_async_remote_copy(
        src_ref=source,
        dst_ref=target,
        send_sem=send_sem,
        recv_sem=recv_sem,
        device_id=device,
        device_id_type=MESH,
    )


def tile_norms(load_tile, count):
    padded = max(count, 16)
    ones = jnp.ones((padded, WIDTH), jnp.bfloat16)
    place = lax.broadcasted_iota(jnp.int32, (padded, TILE), 0)

    def one(tile, found):
        values = load_tile(tile).astype(jnp.float32)
        squares = values * values
        high = squares.astype(jnp.bfloat16)
        low = (squares - high.astype(jnp.float32)).astype(jnp.bfloat16)
        sums = dot_rows(ones, high) + dot_rows(ones, low)
        return jnp.where(place == tile, sums, found)

    found = lax.fori_loop(0, count, one, jnp.zeros((padded, TILE), jnp.float32))
    return found[:count]


def dot_rows(left, right):
    return lax.dot_general(
        left, right, (((1,), (1,)), ((), ())), preferred_element_type=jnp.float32
    )


def spread(values, spread_ref):
    turned = values.T
    for tile in range(values.shape[0]):
        spread_ref[tile] = jnp.broadcast_to(turned[:, tile : tile + 1], (TILE, TILE))


def log_sum(parts):
    peak = jnp.max(parts, axis=0)
    return peak + jnp.log2(jnp.sum(jnp.exp2(parts - peak[None]), axis=0))


def kernel(
    samples,
    references,
    sample_mass,
    reference_mass,
    start,
    pairs,
    counts,
    sample_out,
    reference_out,
    row_buf,
    column_buf,
    column_major,
    row_major,
    column_spread,
    row_spread,
    slot_peak,
    slot_total,
    row_bias,
    column_bias,
    y_buf,
    x_buf,
    z_buf,
    own_sem,
    ring_send,
    ring_recv,
    gather_send,
    gather_recv,
    y_send,
    y_recv,
    x_send,
    x_recv,
    z_send,
    z_recv,
):
    row = lax.axis_index("rows")
    y = lax.axis_index("cols")
    x = lax.div(row, 16)
    z = lax.rem(lax.div(row, 2), 8)
    core = lax.rem(row, 2)
    corner = x * 2 + core

    def at(px, pz, pcore):
        return ((px * 8 + pz) * 2 + pcore, y)

    def y_peer(step):
        return (row, lax.rem(y + step, 8))

    def z_peer(step):
        return at(x, lax.rem(z + step, 8), core)

    def corner_peer(step):
        other = lax.rem(corner + step, 8)
        return at(lax.div(other, 2), z, lax.rem(other, 2))

    barrier = pltpu.get_barrier_semaphore()
    for step in FAR_FIRST:
        for peer in (y_peer(step), z_peer(step), corner_peer(step)):
            pl.semaphore_signal(barrier, inc=1, device_id=peer, device_id_type=MESH)

    def block_of(px, pz, pcore):
        return column_buf.at[px * 2 + lax.div(pz, 4), lax.rem(pz, 4), pcore]

    own_copies = [
        pltpu.make_async_copy(
            samples.at[pl.ds(64 * piece, 64)],
            row_buf.at[2 * y + piece // 2, piece % 2],
            own_sem.at[piece],
        )
        for piece in range(PIECES)
    ]
    own_copies.append(
        pltpu.make_async_copy(references, block_of(x, z, core), own_sem.at[PIECES])
    )
    for copy in own_copies:
        copy.start()

    in_use = counts[0, 0]
    row_place = lax.broadcasted_iota(jnp.int32, (ROW_TILES, TILE), 0)
    column_place = lax.broadcasted_iota(jnp.int32, (COLUMN_TILES, TILE), 0)

    def mark(slot, carry):
        spare = jnp.where(slot < in_use, 0.0, LOWEST).astype(jnp.float32)
        row_bias[slot] = jnp.where(row_place == pairs[0, 0, 0, slot], spare, LOWEST)
        column_bias[slot] = jnp.where(column_place == pairs[0, 0, 1, slot], spare, LOWEST)
        return carry

    lax.fori_loop(0, SLOTS, mark, 0)

    pl.semaphore_wait(barrier, 21)

    def gather(source, target, index, device):
        copy = remote(source, target, gather_send.at[*index], gather_recv.at[*index], device)
        copy.start()
        return copy

    z_copies = {
        step: gather(references, block_of(x, z, core), (0, step), z_peer(step))
        for step in (1, 7, 2, 6, 3, 5, 4)
    }
    x_copies = {}

    def forward(step):
        origin = lax.rem(z + (8 - step), 8)
        landing = block_of(x, origin, core)
        for x_step in (2, 1, 3):
            x_copies[x_step, step] = gather(
                references if step == 0 else landing,
                landing,
                (x_step, step),
                at(lax.rem(x + x_step, 4), z, core),
            )

    ring = {}

    def ring_start(hop, turn):
        for side in (0, 1):
            back = hop - 1
            piece = turn if side == 0 else PIECES - 1 - turn
            block = lax.rem(y + (8 - back if side == 0 else back), 8)
            landing = row_buf.at[2 * block + piece // 2, piece % 2]
            source = samples.at[pl.ds(64 * piece, 64)] if hop == 1 else landing
            copy = remote(
                source,
                landing,
                ring_send.at[side, back, turn],
                ring_recv.at[side, back, turn],
                y_peer(1 if side == 0 else 7),
            )
            copy.start()
            ring[side, hop, turn] = copy

    def ring_wait(hop, turn):
        for side in (0, 1):
            ring[side, hop, turn].wait_recv()

    def ring_turn(hop, turn):
        ring_wait(hop, turn)
        if hop < 3 or (hop == 3 and turn < PIECES // 2):
            ring_start(hop + 1, turn)

    for turn in range(PIECES):
        ring_start(1, turn)
    forward(0)

    for turn, steps in enumerate(((1, 7), (2, 6), (3, 5), (4,))):
        for step in steps:
            z_copies[step].wait_recv()
            forward(step)
        ring_turn(1, turn)
    for copy in own_copies:
        copy.wait()

    core_copies = []

    def swap(step):
        group = lax.rem(x + (4 - step), 4)
        mine = column_buf.at[pl.ds(2 * group, 2), :, core]
        core_copies.append(gather(mine, mine, (4, step), at(x, z, 1 - core)))

    def row_tile(tile):
        return row_buf[tile].reshape(TILE, WIDTH)

    def column_tile(tile):
        return column_buf[tile].reshape(TILE, WIDTH)

    def multiply(steps, groups):
        for step in steps:
            first = 2 * lax.rem(y + step, 8)
            row_values = row_buf[pl.ds(first, 2)].reshape(2 * TILE, WIDTH)
            for group in groups:
                pair = lax.rem(x + (4 - group), 4)
                column_values = column_buf[pl.ds(2 * pair, 2)].reshape(2 * TILE, WIDTH)
                by_column = (2.0 * SCALE) * dot_rows(column_values, row_values)
                by_row = (2.0 * SCALE) * dot_rows(row_values, column_values)
                for i in (0, 1):
                    for j in (0, 1):
                        rows = slice(i * TILE, (i + 1) * TILE)
                        columns = slice(j * TILE, (j + 1) * TILE)
                        place = (first + i) * COLUMN_TILES + 2 * pair + j
                        column_major[place] = by_column[columns, rows]
                        row_major[place] = by_row[rows, columns]

    swap(0)
    ring_turn(2, 0)
    core_copies[0].wait_recv()
    multiply((0, 1, 7), (0,))
    for turn, x_step in enumerate((1, 3, 2)):
        for step in range(8):
            x_copies[x_step, step].wait_recv()
        swap(x_step)
        ring_turn(2, turn + 1)
    multiply((2, 6), (0,))
    core_copies[1].wait_recv()
    multiply((0, 1, 7), (1,))
    ring_turn(3, 0)
    core_copies[2].wait_recv()
    multiply((0, 1, 7), (3,))
    ring_turn(3, 1)
    core_copies[3].wait_recv()
    multiply((0, 1, 7), (2,))
    column_norms = tile_norms(column_tile, COLUMN_TILES)
    spread(SCALE * (start[...] - column_norms), column_spread)
    ring_turn(3, 2)
    multiply((2, 6), (1, 2, 3))
    ring_turn(3, 3)
    multiply((3, 5), (0, 1, 2, 3))
    ring_wait(4, 0)
    ring_wait(4, 1)
    multiply((4,), (0, 1, 2, 3))

    def local_pass(products, spread_ref, axis, bias):
        def one(slot, carry):
            row_id = pairs[0, 0, 0, slot]
            column_id = pairs[0, 0, 1, slot]
            place = row_id * COLUMN_TILES + column_id
            scores = products[place] + spread_ref[column_id if axis else row_id]
            peak = jnp.max(scores, axis=0, keepdims=True)
            slot_peak[pl.ds(slot, 1), :] = peak
            slot_total[pl.ds(slot, 1), :] = jnp.sum(
                jnp.exp2(scores - peak), axis=0, keepdims=True
            )
            return carry

        lax.fori_loop(0, SLOTS, one, 0, unroll=4)
        slot_peak[...] = slot_peak[...] + jnp.log2(slot_total[...])

        shape = bias.shape[1:]

        def highest(slot, peak):
            return jnp.maximum(peak, slot_peak[pl.ds(slot, 1), :] + bias[slot])

        peak = lax.fori_loop(
            0, SLOTS, highest, jnp.full(shape, LOWEST, jnp.float32), unroll=8
        )

        def collect(slot, total):
            return total + jnp.exp2(slot_peak[pl.ds(slot, 1), :] + bias[slot] - peak)

        total = lax.fori_loop(
            0, SLOTS, collect, jnp.zeros(shape, jnp.float32), unroll=8
        )
        return peak + jnp.log2(total)

    def exchange(value, buf, iteration, place, peer, send_sem, recv_sem):
        buf[iteration, place] = value
        copies = []
        for step in FAR_FIRST:
            mine = buf.at[iteration, place]
            copy = remote(
                mine,
                mine,
                send_sem.at[iteration, step],
                recv_sem.at[iteration, step],
                peer(step),
            )
            copy.start()
            copies.append(copy)
        return copies

    def finish(copies, buf, iteration):
        for copy in copies:
            copy.wait()
        return log_sum(buf[iteration])

    sample_logs = jnp.log2(sample_mass[...])
    reference_logs = jnp.log2(reference_mass[...])
    for iteration in range(ITERS):
        value = local_pass(column_major, column_spread, 1, row_bias)
        copies = exchange(value, y_buf, iteration, y, y_peer, y_send, y_recv)
        if iteration == 0:
            row_norms = tile_norms(row_tile, ROW_TILES)
        row_level = sample_logs - finish(copies, y_buf, iteration)
        spread(row_level, row_spread)
        if iteration == ITERS - 1:
            sample_out[...] = row_level * (1.0 / SCALE) + row_norms
        value = local_pass(row_major, row_spread, 0, column_bias)
        copies = exchange(value, x_buf, iteration, corner, corner_peer, x_send, x_recv)
        value = finish(copies, x_buf, iteration)
        copies = exchange(value, z_buf, iteration, z, z_peer, z_send, z_recv)
        column_level = reference_logs - finish(copies, z_buf, iteration)
        if iteration < ITERS - 1:
            spread(column_level, column_spread)
        else:
            reference_out[...] = column_level * (1.0 / SCALE) + column_norms

    for copy in ring.values():
        copy.wait_send()
    for copy in [*z_copies.values(), *x_copies.values(), *core_copies]:
        copy.wait_send()


def body(
    sample_embeddings,
    reference_embeddings,
    sample_mass,
    reference_mass,
    start_potential,
    tile_pairs,
    tile_counts,
):
    vmem = pl.BlockSpec(memory_space=pltpu.VMEM)
    smem = pl.BlockSpec(memory_space=pltpu.SMEM)
    anywhere = pl.BlockSpec(memory_space=pl.ANY)
    dma = pltpu.SemaphoreType.DMA
    sample_out, reference_out = pl.pallas_call(
        kernel,
        out_shape=(
            jax.ShapeDtypeStruct((ROW_TILES, TILE), jnp.float32),
            jax.ShapeDtypeStruct((COLUMN_TILES, TILE), jnp.float32),
        ),
        in_specs=[anywhere, anywhere, vmem, vmem, vmem, smem, smem],
        out_specs=(vmem, vmem),
        scratch_shapes=[
            pltpu.VMEM((ROW_TILES, 2, 64, WIDTH), jnp.bfloat16),
            pltpu.VMEM((COLUMN_TILES, 4, 2, 16, WIDTH), jnp.bfloat16),
            pltpu.VMEM((ROW_TILES * COLUMN_TILES, TILE, TILE), jnp.float32),
            pltpu.VMEM((ROW_TILES * COLUMN_TILES, TILE, TILE), jnp.float32),
            pltpu.VMEM((COLUMN_TILES, TILE, TILE), jnp.float32),
            pltpu.VMEM((ROW_TILES, TILE, TILE), jnp.float32),
            pltpu.VMEM((SLOTS, TILE), jnp.float32),
            pltpu.VMEM((SLOTS, TILE), jnp.float32),
            pltpu.VMEM((SLOTS, ROW_TILES, TILE), jnp.float32),
            pltpu.VMEM((SLOTS, COLUMN_TILES, TILE), jnp.float32),
            pltpu.VMEM((ITERS, 8, ROW_TILES, TILE), jnp.float32),
            pltpu.VMEM((ITERS, 8, COLUMN_TILES, TILE), jnp.float32),
            pltpu.VMEM((ITERS, 8, COLUMN_TILES, TILE), jnp.float32),
            dma((PIECES + 1,)),
            dma((2, 4, PIECES)),
            dma((2, 4, PIECES)),
            dma((5, 8)),
            dma((5, 8)),
            dma((ITERS, 8)),
            dma((ITERS, 8)),
            dma((ITERS, 8)),
            dma((ITERS, 8)),
            dma((ITERS, 8)),
            dma((ITERS, 8)),
        ],
        compiler_params=pltpu.CompilerParams(collective_id=0, has_side_effects=True),
    )(
        sample_embeddings,
        reference_embeddings,
        sample_mass.reshape(ROW_TILES, TILE),
        reference_mass.reshape(COLUMN_TILES, TILE),
        start_potential.reshape(COLUMN_TILES, TILE),
        tile_pairs,
        tile_counts,
    )
    return (sample_out.reshape(-1), reference_out.reshape(-1))


def solution(mesh):
    placed = (
        P(("rows", "cols"), None),
        P(("cols", "rows"), None),
        P("rows"),
        P("cols"),
        P("cols"),
        P("rows", "cols", None, None),
        P("rows", "cols"),
    )
    return jax.shard_map(
        body, mesh=mesh, in_specs=placed, out_specs=(P("rows"), P("cols")), check_vma=False
    )
```

```python
import math

import jax
import jax.numpy as jnp
from jax import lax
from jax.experimental import pallas as pl
from jax.experimental.pallas import tpu as pltpu
from jax.sharding import PartitionSpec as P

TILE = 128
ITERS = 2
WIDTH = 256
ROW_TILES = 16
COLUMN_TILES = 8
SLOTS = 48
PIECES = 4
FAR_FIRST = (4, 3, 5, 2, 6, 1, 7)

SCALE = math.log2(math.e) / 0.1
LOWEST = -1e30
MESH = pl.DeviceIdType.MESH


def remote(source, target, send_sem, recv_sem, device):
    return pltpu.make_async_remote_copy(
        src_ref=source,
        dst_ref=target,
        send_sem=send_sem,
        recv_sem=recv_sem,
        device_id=device,
        device_id_type=MESH,
    )


def tile_norms(load_tile, count):
    padded = max(count, 16)
    ones = jnp.ones((padded, WIDTH), jnp.bfloat16)
    place = lax.broadcasted_iota(jnp.int32, (padded, TILE), 0)

    def one(tile, found):
        values = load_tile(tile).astype(jnp.float32)
        squares = values * values
        high = squares.astype(jnp.bfloat16)
        low = (squares - high.astype(jnp.float32)).astype(jnp.bfloat16)
        sums = dot_rows(ones, high) + dot_rows(ones, low)
        return jnp.where(place == tile, sums, found)

    found = lax.fori_loop(0, count, one, jnp.zeros((padded, TILE), jnp.float32))
    return found[:count]


def dot_rows(left, right):
    return lax.dot_general(
        left, right, (((1,), (1,)), ((), ())), preferred_element_type=jnp.float32
    )


def spread(values, spread_ref):
    turned = values.T
    for tile in range(values.shape[0]):
        spread_ref[tile] = jnp.broadcast_to(turned[:, tile : tile + 1], (TILE, TILE))


def log_sum(parts):
    peak = jnp.max(parts, axis=0)
    return peak + jnp.log2(jnp.sum(jnp.exp2(parts - peak[None]), axis=0))


def kernel(
    samples,
    references,
    sample_mass,
    reference_mass,
    start,
    pairs,
    counts,
    sample_out,
    reference_out,
    row_buf,
    column_buf,
    column_major,
    row_major,
    column_spread,
    row_spread,
    slot_peak,
    slot_total,
    row_bias,
    column_bias,
    y_buf,
    x_buf,
    z_buf,
    own_sem,
    ring_send,
    ring_recv,
    gather_send,
    gather_recv,
    y_send,
    y_recv,
    x_send,
    x_recv,
    z_send,
    z_recv,
):
    row = lax.axis_index("rows")
    y = lax.axis_index("cols")
    x = lax.div(row, 16)
    z = lax.rem(lax.div(row, 2), 8)
    core = lax.rem(row, 2)
    corner = x * 2 + core

    def at(px, pz, pcore):
        return ((px * 8 + pz) * 2 + pcore, y)

    def y_peer(step):
        return (row, lax.rem(y + step, 8))

    def z_peer(step):
        return at(x, lax.rem(z + step, 8), core)

    def corner_peer(step):
        other = lax.rem(corner + step, 8)
        return at(lax.div(other, 2), z, lax.rem(other, 2))

    barrier = pltpu.get_barrier_semaphore()
    for step in FAR_FIRST:
        for peer in (y_peer(step), z_peer(step), corner_peer(step)):
            pl.semaphore_signal(barrier, inc=1, device_id=peer, device_id_type=MESH)

    def block_of(px, pz, pcore):
        return column_buf.at[px * 2 + lax.div(pz, 4), lax.rem(pz, 4), pcore]

    own_copies = [
        pltpu.make_async_copy(
            samples.at[pl.ds(64 * piece, 64)],
            row_buf.at[2 * y + piece // 2, piece % 2],
            own_sem.at[piece],
        )
        for piece in range(PIECES)
    ]
    own_copies.append(
        pltpu.make_async_copy(references, block_of(x, z, core), own_sem.at[PIECES])
    )
    for copy in own_copies:
        copy.start()

    in_use = counts[0, 0]
    row_place = lax.broadcasted_iota(jnp.int32, (ROW_TILES, TILE), 0)
    column_place = lax.broadcasted_iota(jnp.int32, (COLUMN_TILES, TILE), 0)

    def mark(slot, carry):
        spare = jnp.where(slot < in_use, 0.0, LOWEST).astype(jnp.float32)
        row_bias[slot] = jnp.where(row_place == pairs[0, 0, 0, slot], spare, LOWEST)
        column_bias[slot] = jnp.where(column_place == pairs[0, 0, 1, slot], spare, LOWEST)
        return carry

    lax.fori_loop(0, SLOTS, mark, 0)
    spread(SCALE * start[...], column_spread)

    pl.semaphore_wait(barrier, 21)

    def gather(source, target, index, device):
        copy = remote(source, target, gather_send.at[*index], gather_recv.at[*index], device)
        copy.start()
        return copy

    z_copies = {
        step: gather(references, block_of(x, z, core), (0, step), z_peer(step))
        for step in (1, 7, 2, 6, 3, 5, 4)
    }
    x_copies = {}

    def forward(step):
        origin = lax.rem(z + (8 - step), 8)
        landing = block_of(x, origin, core)
        for x_step in (2, 1, 3):
            x_copies[x_step, step] = gather(
                references if step == 0 else landing,
                landing,
                (x_step, step),
                at(lax.rem(x + x_step, 4), z, core),
            )

    ring = {}

    def ring_start(hop, turn):
        for side in (0, 1):
            back = hop - 1
            piece = turn if side == 0 else PIECES - 1 - turn
            block = lax.rem(y + (8 - back if side == 0 else back), 8)
            landing = row_buf.at[2 * block + piece // 2, piece % 2]
            source = samples.at[pl.ds(64 * piece, 64)] if hop == 1 else landing
            copy = remote(
                source,
                landing,
                ring_send.at[side, back, turn],
                ring_recv.at[side, back, turn],
                y_peer(1 if side == 0 else 7),
            )
            copy.start()
            ring[side, hop, turn] = copy

    def ring_wait(hop, turn):
        for side in (0, 1):
            ring[side, hop, turn].wait_recv()

    def ring_turn(hop, turn):
        ring_wait(hop, turn)
        if hop < 3 or (hop == 3 and turn < PIECES // 2):
            ring_start(hop + 1, turn)

    for turn in range(PIECES):
        ring_start(1, turn)
    forward(0)

    for turn, steps in enumerate(((1, 7), (2, 6), (3, 5), (4,))):
        for step in steps:
            z_copies[step].wait_recv()
            forward(step)
        ring_turn(1, turn)
    for copy in own_copies:
        copy.wait()

    core_copies = []

    def swap(step):
        group = lax.rem(x + (4 - step), 4)
        mine = column_buf.at[pl.ds(2 * group, 2), :, core]
        core_copies.append(gather(mine, mine, (4, step), at(x, z, 1 - core)))

    def row_tile(tile):
        return row_buf[tile].reshape(TILE, WIDTH)

    def column_tile(tile):
        return column_buf[tile].reshape(TILE, WIDTH)

    def multiply(steps, groups):
        for step in steps:
            first = 2 * lax.rem(y + step, 8)
            row_values = row_buf[pl.ds(first, 2)].reshape(2 * TILE, WIDTH)
            for group in groups:
                pair = lax.rem(x + (4 - group), 4)
                column_values = column_buf[pl.ds(2 * pair, 2)].reshape(2 * TILE, WIDTH)
                by_column = (2.0 * SCALE) * dot_rows(column_values, row_values)
                by_row = (2.0 * SCALE) * dot_rows(row_values, column_values)
                for i in (0, 1):
                    for j in (0, 1):
                        rows = slice(i * TILE, (i + 1) * TILE)
                        columns = slice(j * TILE, (j + 1) * TILE)
                        place = (first + i) * COLUMN_TILES + 2 * pair + j
                        column_major[place] = by_column[columns, rows]
                        row_major[place] = by_row[rows, columns]

    def level(group):
        for half in (0, 1):
            tile = 2 * lax.rem(x + (4 - group), 4) + half
            values = column_tile(tile).astype(jnp.float32)
            norms = jnp.sum(values * values, axis=1, keepdims=True)
            column_spread[tile] = column_spread[tile] - SCALE * norms

    swap(0)
    ring_turn(2, 0)
    core_copies[0].wait_recv()
    multiply((0, 1, 7), (0,))
    level(0)
    ring_turn(2, 1)
    ring_turn(2, 2)
    ring_turn(2, 3)
    for x_step in (1, 3, 2):
        for step in range(8):
            x_copies[x_step, step].wait_recv()
        swap(x_step)
    multiply((2, 6), (0,))
    ring_turn(3, 0)
    core_copies[1].wait_recv()
    multiply((0, 1, 7), (1,))
    level(1)
    ring_turn(3, 1)
    core_copies[2].wait_recv()
    multiply((0, 1, 7), (3,))
    level(3)
    core_copies[3].wait_recv()
    multiply((0, 1, 7), (2,))
    level(2)
    multiply((2, 6), (1, 3, 2))
    ring_turn(3, 2)
    ring_turn(3, 3)
    multiply((3, 5), (0, 1, 2, 3))
    ring_wait(4, 0)
    ring_wait(4, 1)
    multiply((4,), (0, 1, 2, 3))

    def local_pass(products, spread_ref, axis, bias):
        def one(slot, carry):
            row_id = pairs[0, 0, 0, slot]
            column_id = pairs[0, 0, 1, slot]
            place = row_id * COLUMN_TILES + column_id
            scores = products[place] + spread_ref[column_id if axis else row_id]
            peak = jnp.max(scores, axis=0, keepdims=True)
            slot_peak[pl.ds(slot, 1), :] = peak
            slot_total[pl.ds(slot, 1), :] = jnp.sum(
                jnp.exp2(scores - peak), axis=0, keepdims=True
            )
            return carry

        lax.fori_loop(0, SLOTS, one, 0, unroll=16)
        slot_peak[...] = slot_peak[...] + jnp.log2(slot_total[...])

        shape = bias.shape[1:]

        def highest(slot, peak):
            return jnp.maximum(peak, slot_peak[pl.ds(slot, 1), :] + bias[slot])

        peak = lax.fori_loop(
            0, SLOTS, highest, jnp.full(shape, LOWEST, jnp.float32), unroll=8
        )

        def collect(slot, total):
            return total + jnp.exp2(slot_peak[pl.ds(slot, 1), :] + bias[slot] - peak)

        total = lax.fori_loop(
            0, SLOTS, collect, jnp.zeros(shape, jnp.float32), unroll=8
        )
        return peak + jnp.log2(total)

    def exchange(value, buf, iteration, place, peer, send_sem, recv_sem):
        buf[iteration, place] = value
        copies = []
        for step in FAR_FIRST:
            mine = buf.at[iteration, place]
            copy = remote(
                mine,
                mine,
                send_sem.at[iteration, step],
                recv_sem.at[iteration, step],
                peer(step),
            )
            copy.start()
            copies.append(copy)
        return copies

    def finish(copies, buf, iteration):
        for copy in copies:
            copy.wait()
        return log_sum(buf[iteration])

    sample_logs = jnp.log2(sample_mass[...])
    reference_logs = jnp.log2(reference_mass[...])
    for iteration in range(ITERS):
        value = local_pass(column_major, column_spread, 1, row_bias)
        copies = exchange(value, y_buf, iteration, y, y_peer, y_send, y_recv)
        if iteration == 0:
            row_norms = tile_norms(row_tile, ROW_TILES)
        row_level = sample_logs - finish(copies, y_buf, iteration)
        spread(row_level, row_spread)
        if iteration == ITERS - 1:
            sample_out[...] = row_level * (1.0 / SCALE) + row_norms
        value = local_pass(row_major, row_spread, 0, column_bias)
        copies = exchange(value, x_buf, iteration, corner, corner_peer, x_send, x_recv)
        value = finish(copies, x_buf, iteration)
        copies = exchange(value, z_buf, iteration, z, z_peer, z_send, z_recv)
        if iteration == 0:
            column_norms = tile_norms(column_tile, COLUMN_TILES)
        column_level = reference_logs - finish(copies, z_buf, iteration)
        if iteration < ITERS - 1:
            spread(column_level, column_spread)
        else:
            reference_out[...] = column_level * (1.0 / SCALE) + column_norms

    for copy in ring.values():
        copy.wait_send()
    for copy in [*z_copies.values(), *x_copies.values(), *core_copies]:
        copy.wait_send()


def deliver(sample_ref, reference_ref, sample_out, reference_out):
    sample_out[...] = sample_ref[...]
    reference_out[...] = reference_ref[...]


def body(
    sample_embeddings,
    reference_embeddings,
    sample_mass,
    reference_mass,
    start_potential,
    tile_pairs,
    tile_counts,
):
    vmem = pl.BlockSpec(memory_space=pltpu.VMEM)
    smem = pl.BlockSpec(memory_space=pltpu.SMEM)
    anywhere = pl.BlockSpec(memory_space=pl.ANY)
    dma = pltpu.SemaphoreType.DMA
    sample_out, reference_out = pl.pallas_call(
        kernel,
        out_shape=(
            jax.ShapeDtypeStruct((ROW_TILES, TILE), jnp.float32),
            jax.ShapeDtypeStruct((COLUMN_TILES, TILE), jnp.float32),
        ),
        in_specs=[anywhere, anywhere, vmem, vmem, vmem, smem, smem],
        out_specs=(vmem, vmem),
        scratch_shapes=[
            pltpu.VMEM((ROW_TILES, 2, 64, WIDTH), jnp.bfloat16),
            pltpu.VMEM((COLUMN_TILES, 4, 2, 16, WIDTH), jnp.bfloat16),
            pltpu.VMEM((ROW_TILES * COLUMN_TILES, TILE, TILE), jnp.float32),
            pltpu.VMEM((ROW_TILES * COLUMN_TILES, TILE, TILE), jnp.float32),
            pltpu.VMEM((COLUMN_TILES, TILE, TILE), jnp.float32),
            pltpu.VMEM((ROW_TILES, TILE, TILE), jnp.float32),
            pltpu.VMEM((SLOTS, TILE), jnp.float32),
            pltpu.VMEM((SLOTS, TILE), jnp.float32),
            pltpu.VMEM((SLOTS, ROW_TILES, TILE), jnp.float32),
            pltpu.VMEM((SLOTS, COLUMN_TILES, TILE), jnp.float32),
            pltpu.VMEM((ITERS, 8, ROW_TILES, TILE), jnp.float32),
            pltpu.VMEM((ITERS, 8, COLUMN_TILES, TILE), jnp.float32),
            pltpu.VMEM((ITERS, 8, COLUMN_TILES, TILE), jnp.float32),
            dma((PIECES + 1,)),
            dma((2, 4, PIECES)),
            dma((2, 4, PIECES)),
            dma((5, 8)),
            dma((5, 8)),
            dma((ITERS, 8)),
            dma((ITERS, 8)),
            dma((ITERS, 8)),
            dma((ITERS, 8)),
            dma((ITERS, 8)),
            dma((ITERS, 8)),
        ],
        compiler_params=pltpu.CompilerParams(collective_id=0, has_side_effects=True),
    )(
        sample_embeddings,
        reference_embeddings,
        sample_mass.reshape(ROW_TILES, TILE),
        reference_mass.reshape(COLUMN_TILES, TILE),
        start_potential.reshape(COLUMN_TILES, TILE),
        tile_pairs,
        tile_counts,
    )
    sample_out, reference_out = pl.pallas_call(
        deliver,
        out_shape=(
            jax.ShapeDtypeStruct((ROW_TILES, TILE), jnp.float32),
            jax.ShapeDtypeStruct((COLUMN_TILES, TILE), jnp.float32),
        ),
        in_specs=[vmem, vmem],
        out_specs=(vmem, vmem),
    )(sample_out, reference_out)
    return (sample_out.reshape(-1), reference_out.reshape(-1))


def solution(mesh):
    placed = (
        P(("rows", "cols"), None),
        P(("cols", "rows"), None),
        P("rows"),
        P("cols"),
        P("cols"),
        P("rows", "cols", None, None),
        P("rows", "cols"),
    )
    return jax.shard_map(
        body, mesh=mesh, in_specs=placed, out_specs=(P("rows"), P("cols")), check_vma=False
    )
```

```python
import math

import jax
import jax.numpy as jnp
from jax import lax
from jax.experimental import pallas as pl
from jax.experimental.pallas import tpu as pltpu
from jax.sharding import PartitionSpec as P

TILE = 128
ITERS = 2
WIDTH = 256
ROW_TILES = 16
COLUMN_TILES = 8
SLOTS = 48
PIECES = 4
FAR_FIRST = (4, 3, 5, 2, 6, 1, 7)

SCALE = math.log2(math.e) / 0.1
LOWEST = -1e30
MESH = pl.DeviceIdType.MESH


def remote(source, target, send_sem, recv_sem, device):
    return pltpu.make_async_remote_copy(
        src_ref=source,
        dst_ref=target,
        send_sem=send_sem,
        recv_sem=recv_sem,
        device_id=device,
        device_id_type=MESH,
    )


def tile_norms(load_tile, count):
    padded = max(count, 16)
    ones = jnp.ones((padded, WIDTH), jnp.bfloat16)
    place = lax.broadcasted_iota(jnp.int32, (padded, TILE), 0)

    def one(tile, found):
        values = load_tile(tile).astype(jnp.float32)
        squares = values * values
        high = squares.astype(jnp.bfloat16)
        low = (squares - high.astype(jnp.float32)).astype(jnp.bfloat16)
        sums = dot_rows(ones, high) + dot_rows(ones, low)
        return jnp.where(place == tile, sums, found)

    found = lax.fori_loop(0, count, one, jnp.zeros((padded, TILE), jnp.float32))
    return found[:count]


def dot_rows(left, right):
    return lax.dot_general(
        left, right, (((1,), (1,)), ((), ())), preferred_element_type=jnp.float32
    )


def spread(values, spread_ref):
    turned = values.T
    for tile in range(values.shape[0]):
        spread_ref[tile] = jnp.broadcast_to(turned[:, tile : tile + 1], (TILE, TILE))


def log_sum(parts):
    peak = jnp.max(parts, axis=0)
    return peak + jnp.log2(jnp.sum(jnp.exp2(parts - peak[None]), axis=0))


def kernel(
    samples,
    references,
    sample_mass,
    reference_mass,
    start,
    pairs,
    counts,
    sample_out,
    reference_out,
    row_buf,
    column_buf,
    column_major,
    row_major,
    column_spread,
    row_spread,
    slot_peak,
    slot_total,
    row_bias,
    column_bias,
    y_buf,
    x_buf,
    z_buf,
    own_sem,
    ring_send,
    ring_recv,
    gather_send,
    gather_recv,
    y_send,
    y_recv,
    x_send,
    x_recv,
    z_send,
    z_recv,
):
    row = lax.axis_index("rows")
    y = lax.axis_index("cols")
    x = lax.div(row, 16)
    z = lax.rem(lax.div(row, 2), 8)
    core = lax.rem(row, 2)
    corner = x * 2 + core

    def at(px, pz, pcore):
        return ((px * 8 + pz) * 2 + pcore, y)

    def y_peer(step):
        return (row, lax.rem(y + step, 8))

    def z_peer(step):
        return at(x, lax.rem(z + step, 8), core)

    def corner_peer(step):
        other = lax.rem(corner + step, 8)
        return at(lax.div(other, 2), z, lax.rem(other, 2))

    barrier = pltpu.get_barrier_semaphore()
    for step in FAR_FIRST:
        for peer in (y_peer(step), z_peer(step), corner_peer(step)):
            pl.semaphore_signal(barrier, inc=1, device_id=peer, device_id_type=MESH)

    def block_of(px, pz, pcore):
        return column_buf.at[px * 2 + lax.div(pz, 4), lax.rem(pz, 4), pcore]

    own_copies = [
        pltpu.make_async_copy(
            samples.at[pl.ds(64 * piece, 64)],
            row_buf.at[2 * y + piece // 2, piece % 2],
            own_sem.at[piece],
        )
        for piece in range(PIECES)
    ]
    own_copies.append(
        pltpu.make_async_copy(references, block_of(x, z, core), own_sem.at[PIECES])
    )
    for copy in own_copies:
        copy.start()

    in_use = counts[0, 0]
    row_place = lax.broadcasted_iota(jnp.int32, (ROW_TILES, TILE), 0)
    column_place = lax.broadcasted_iota(jnp.int32, (COLUMN_TILES, TILE), 0)

    def mark(slot, carry):
        spare = jnp.where(slot < in_use, 0.0, LOWEST).astype(jnp.float32)
        row_bias[slot] = jnp.where(row_place == pairs[0, 0, 0, slot], spare, LOWEST)
        column_bias[slot] = jnp.where(column_place == pairs[0, 0, 1, slot], spare, LOWEST)
        return carry

    lax.fori_loop(0, SLOTS, mark, 0)
    spread(SCALE * start[...], column_spread)

    pl.semaphore_wait(barrier, 21)

    def gather(source, target, index, device):
        copy = remote(source, target, gather_send.at[*index], gather_recv.at[*index], device)
        copy.start()
        return copy

    z_copies = {
        step: gather(references, block_of(x, z, core), (0, step), z_peer(step))
        for step in (1, 7, 2, 6, 3, 5, 4)
    }
    x_copies = {}

    def forward(step):
        origin = lax.rem(z + (8 - step), 8)
        landing = block_of(x, origin, core)
        for x_step in (2, 1, 3):
            x_copies[x_step, step] = gather(
                references if step == 0 else landing,
                landing,
                (x_step, step),
                at(lax.rem(x + x_step, 4), z, core),
            )

    ring = {}

    def ring_start(hop, turn):
        for side in (0, 1):
            back = hop - 1
            piece = turn if side == 0 else PIECES - 1 - turn
            block = lax.rem(y + (8 - back if side == 0 else back), 8)
            landing = row_buf.at[2 * block + piece // 2, piece % 2]
            source = samples.at[pl.ds(64 * piece, 64)] if hop == 1 else landing
            copy = remote(
                source,
                landing,
                ring_send.at[side, back, turn],
                ring_recv.at[side, back, turn],
                y_peer(1 if side == 0 else 7),
            )
            copy.start()
            ring[side, hop, turn] = copy

    def ring_wait(hop, turn):
        for side in (0, 1):
            ring[side, hop, turn].wait_recv()

    def ring_turn(hop, turn):
        ring_wait(hop, turn)
        if hop < 3 or (hop == 3 and turn < PIECES // 2):
            ring_start(hop + 1, turn)

    for turn in range(PIECES):
        ring_start(1, turn)
    forward(0)

    for turn, steps in enumerate(((1, 7), (2, 6), (3, 5), (4,))):
        for step in steps:
            z_copies[step].wait_recv()
            forward(step)
        ring_turn(1, turn)
    for copy in own_copies:
        copy.wait()

    core_copies = []

    def swap(step):
        group = lax.rem(x + (4 - step), 4)
        mine = column_buf.at[pl.ds(2 * group, 2), :, core]
        core_copies.append(gather(mine, mine, (4, step), at(x, z, 1 - core)))

    def row_tile(tile):
        return row_buf[tile].reshape(TILE, WIDTH)

    def column_tile(tile):
        return column_buf[tile].reshape(TILE, WIDTH)

    def multiply(steps, groups):
        for step in steps:
            first = 2 * lax.rem(y + step, 8)
            row_values = row_buf[pl.ds(first, 2)].reshape(2 * TILE, WIDTH)
            for group in groups:
                pair = lax.rem(x + (4 - group), 4)
                column_values = column_buf[pl.ds(2 * pair, 2)].reshape(2 * TILE, WIDTH)
                by_column = (2.0 * SCALE) * dot_rows(column_values, row_values)
                by_row = (2.0 * SCALE) * dot_rows(row_values, column_values)
                for i in (0, 1):
                    for j in (0, 1):
                        rows = slice(i * TILE, (i + 1) * TILE)
                        columns = slice(j * TILE, (j + 1) * TILE)
                        place = (first + i) * COLUMN_TILES + 2 * pair + j
                        column_major[place] = by_column[columns, rows]
                        row_major[place] = by_row[rows, columns]

    def level(group):
        for half in (0, 1):
            tile = 2 * lax.rem(x + (4 - group), 4) + half
            values = column_tile(tile).astype(jnp.float32)
            norms = jnp.sum(values * values, axis=1, keepdims=True)
            column_spread[tile] = column_spread[tile] - SCALE * norms

    swap(0)
    ring_turn(2, 0)
    core_copies[0].wait_recv()
    multiply((0, 1, 7), (0,))
    level(0)
    ring_turn(2, 1)
    ring_turn(2, 2)
    ring_turn(2, 3)
    for x_step in (1, 3, 2):
        for step in range(8):
            x_copies[x_step, step].wait_recv()
        swap(x_step)
    multiply((2, 6), (0,))
    ring_turn(3, 0)
    core_copies[1].wait_recv()
    multiply((0, 1, 7), (1,))
    level(1)
    ring_turn(3, 1)
    core_copies[2].wait_recv()
    multiply((0, 1, 7), (3,))
    level(3)
    core_copies[3].wait_recv()
    multiply((0, 1, 7), (2,))
    level(2)
    multiply((2, 6), (1, 3, 2))
    ring_turn(3, 2)
    ring_turn(3, 3)
    multiply((3, 5), (0, 1, 2, 3))
    ring_wait(4, 0)
    ring_wait(4, 1)
    multiply((4,), (0, 1, 2, 3))

    def local_pass(products, spread_ref, axis, bias):
        shape = bias.shape[1:]

        def one(slot, highest):
            row_id = pairs[0, 0, 0, slot]
            column_id = pairs[0, 0, 1, slot]
            place = row_id * COLUMN_TILES + column_id
            scores = products[place] + spread_ref[column_id if axis else row_id]
            peak = jnp.max(scores, axis=0, keepdims=True)
            slot_peak[pl.ds(slot, 1), :] = peak
            slot_total[pl.ds(slot, 1), :] = jnp.sum(
                jnp.exp2(scores - peak), axis=0, keepdims=True
            )
            return jnp.maximum(highest, peak + bias[slot])

        peak = lax.fori_loop(
            0, SLOTS, one, jnp.full(shape, LOWEST, jnp.float32), unroll=48
        )

        def collect(slot, total):
            scale = jnp.exp2(slot_peak[pl.ds(slot, 1), :] + bias[slot] - peak)
            return total + slot_total[pl.ds(slot, 1), :] * scale

        total = lax.fori_loop(
            0, SLOTS, collect, jnp.zeros(shape, jnp.float32), unroll=48
        )
        return peak + jnp.log2(total)

    def exchange(value, buf, iteration, place, peer, send_sem, recv_sem):
        buf[iteration, place] = value
        copies = []
        for step in FAR_FIRST:
            mine = buf.at[iteration, place]
            copy = remote(
                mine,
                mine,
                send_sem.at[iteration, step],
                recv_sem.at[iteration, step],
                peer(step),
            )
            copy.start()
            copies.append(copy)
        return copies

    def finish(copies, buf, iteration):
        for copy in copies:
            copy.wait()
        return log_sum(buf[iteration])

    sample_logs = jnp.log2(sample_mass[...])
    reference_logs = jnp.log2(reference_mass[...])
    for iteration in range(ITERS):
        value = local_pass(column_major, column_spread, 1, row_bias)
        copies = exchange(value, y_buf, iteration, y, y_peer, y_send, y_recv)
        if iteration == 0:
            row_norms = tile_norms(row_tile, ROW_TILES)
        row_level = sample_logs - finish(copies, y_buf, iteration)
        spread(row_level, row_spread)
        if iteration == ITERS - 1:
            sample_out[...] = row_level * (1.0 / SCALE) + row_norms
        value = local_pass(row_major, row_spread, 0, column_bias)
        copies = exchange(value, x_buf, iteration, corner, corner_peer, x_send, x_recv)
        value = finish(copies, x_buf, iteration)
        copies = exchange(value, z_buf, iteration, z, z_peer, z_send, z_recv)
        if iteration == 0:
            column_norms = tile_norms(column_tile, COLUMN_TILES)
        column_level = reference_logs - finish(copies, z_buf, iteration)
        if iteration < ITERS - 1:
            spread(column_level, column_spread)
        else:
            reference_out[...] = column_level * (1.0 / SCALE) + column_norms

    for copy in ring.values():
        copy.wait_send()
    for copy in [*z_copies.values(), *x_copies.values(), *core_copies]:
        copy.wait_send()


def deliver(sample_ref, reference_ref, sample_out, reference_out):
    sample_out[...] = sample_ref[...]
    reference_out[...] = reference_ref[...]


def body(
    sample_embeddings,
    reference_embeddings,
    sample_mass,
    reference_mass,
    start_potential,
    tile_pairs,
    tile_counts,
):
    vmem = pl.BlockSpec(memory_space=pltpu.VMEM)
    smem = pl.BlockSpec(memory_space=pltpu.SMEM)
    anywhere = pl.BlockSpec(memory_space=pl.ANY)
    dma = pltpu.SemaphoreType.DMA
    sample_out, reference_out = pl.pallas_call(
        kernel,
        out_shape=(
            jax.ShapeDtypeStruct((ROW_TILES, TILE), jnp.float32),
            jax.ShapeDtypeStruct((COLUMN_TILES, TILE), jnp.float32),
        ),
        in_specs=[anywhere, anywhere, vmem, vmem, vmem, smem, smem],
        out_specs=(vmem, vmem),
        scratch_shapes=[
            pltpu.VMEM((ROW_TILES, 2, 64, WIDTH), jnp.bfloat16),
            pltpu.VMEM((COLUMN_TILES, 4, 2, 16, WIDTH), jnp.bfloat16),
            pltpu.VMEM((ROW_TILES * COLUMN_TILES, TILE, TILE), jnp.float32),
            pltpu.VMEM((ROW_TILES * COLUMN_TILES, TILE, TILE), jnp.float32),
            pltpu.VMEM((COLUMN_TILES, TILE, TILE), jnp.float32),
            pltpu.VMEM((ROW_TILES, TILE, TILE), jnp.float32),
            pltpu.VMEM((SLOTS, TILE), jnp.float32),
            pltpu.VMEM((SLOTS, TILE), jnp.float32),
            pltpu.VMEM((SLOTS, ROW_TILES, TILE), jnp.float32),
            pltpu.VMEM((SLOTS, COLUMN_TILES, TILE), jnp.float32),
            pltpu.VMEM((ITERS, 8, ROW_TILES, TILE), jnp.float32),
            pltpu.VMEM((ITERS, 8, COLUMN_TILES, TILE), jnp.float32),
            pltpu.VMEM((ITERS, 8, COLUMN_TILES, TILE), jnp.float32),
            dma((PIECES + 1,)),
            dma((2, 4, PIECES)),
            dma((2, 4, PIECES)),
            dma((5, 8)),
            dma((5, 8)),
            dma((ITERS, 8)),
            dma((ITERS, 8)),
            dma((ITERS, 8)),
            dma((ITERS, 8)),
            dma((ITERS, 8)),
            dma((ITERS, 8)),
        ],
        compiler_params=pltpu.CompilerParams(collective_id=0, has_side_effects=True),
    )(
        sample_embeddings,
        reference_embeddings,
        sample_mass.reshape(ROW_TILES, TILE),
        reference_mass.reshape(COLUMN_TILES, TILE),
        start_potential.reshape(COLUMN_TILES, TILE),
        tile_pairs,
        tile_counts,
    )
    sample_out, reference_out = pl.pallas_call(
        deliver,
        out_shape=(
            jax.ShapeDtypeStruct((ROW_TILES, TILE), jnp.float32),
            jax.ShapeDtypeStruct((COLUMN_TILES, TILE), jnp.float32),
        ),
        in_specs=[vmem, vmem],
        out_specs=(vmem, vmem),
    )(sample_out, reference_out)
    return (sample_out.reshape(-1), reference_out.reshape(-1))


def solution(mesh):
    placed = (
        P(("rows", "cols"), None),
        P(("cols", "rows"), None),
        P("rows"),
        P("cols"),
        P("cols"),
        P("rows", "cols", None, None),
        P("rows", "cols"),
    )
    return jax.shard_map(
        body, mesh=mesh, in_specs=placed, out_specs=(P("rows"), P("cols")), check_vma=False
    )
```

```python
import math

import jax
import jax.numpy as jnp
from jax import lax
from jax.experimental import pallas as pl
from jax.experimental.pallas import tpu as pltpu
from jax.sharding import PartitionSpec as P

TILE = 128
ITERS = 2
WIDTH = 256
ROW_TILES = 16
COLUMN_TILES = 8
SLOTS = 48
PIECES = 4
FAR_FIRST = (4, 3, 5, 2, 6, 1, 7)

SCALE = math.log2(math.e) / 0.1
LOWEST = -1e30
MESH = pl.DeviceIdType.MESH


def remote(source, target, send_sem, recv_sem, device):
    return pltpu.make_async_remote_copy(
        src_ref=source,
        dst_ref=target,
        send_sem=send_sem,
        recv_sem=recv_sem,
        device_id=device,
        device_id_type=MESH,
    )


def tile_norms(load_tile, count):
    padded = max(count, 16)
    ones = jnp.ones((padded, WIDTH), jnp.bfloat16)
    place = lax.broadcasted_iota(jnp.int32, (padded, TILE), 0)

    def one(tile, found):
        values = load_tile(tile).astype(jnp.float32)
        squares = values * values
        high = squares.astype(jnp.bfloat16)
        low = (squares - high.astype(jnp.float32)).astype(jnp.bfloat16)
        sums = dot_rows(ones, high) + dot_rows(ones, low)
        return jnp.where(place == tile, sums, found)

    found = lax.fori_loop(0, count, one, jnp.zeros((padded, TILE), jnp.float32))
    return found[:count]


def dot_rows(left, right):
    return lax.dot_general(
        left, right, (((1,), (1,)), ((), ())), preferred_element_type=jnp.float32
    )


def spread(values, spread_ref):
    turned = values.T
    for tile in range(values.shape[0]):
        spread_ref[tile] = jnp.broadcast_to(turned[:, tile : tile + 1], (TILE, TILE))


def log_sum(parts):
    peak = jnp.max(parts, axis=0)
    return peak + jnp.log2(jnp.sum(jnp.exp2(parts - peak[None]), axis=0))


def kernel(
    samples,
    references,
    sample_mass,
    reference_mass,
    start,
    pairs,
    counts,
    sample_out,
    reference_out,
    row_buf,
    column_buf,
    column_major,
    row_major,
    column_spread,
    row_spread,
    slot_peak,
    slot_total,
    row_bias,
    column_bias,
    y_buf,
    x_buf,
    z_buf,
    own_sem,
    ring_send,
    ring_recv,
    gather_send,
    gather_recv,
    y_send,
    y_recv,
    x_send,
    x_recv,
    z_send,
    z_recv,
):
    row = lax.axis_index("rows")
    y = lax.axis_index("cols")
    x = lax.div(row, 16)
    z = lax.rem(lax.div(row, 2), 8)
    core = lax.rem(row, 2)
    corner = x * 2 + core

    def at(px, pz, pcore):
        return ((px * 8 + pz) * 2 + pcore, y)

    def y_peer(step):
        return (row, lax.rem(y + step, 8))

    def z_peer(step):
        return at(x, lax.rem(z + step, 8), core)

    def corner_peer(step):
        other = lax.rem(corner + step, 8)
        return at(lax.div(other, 2), z, lax.rem(other, 2))

    barrier = pltpu.get_barrier_semaphore()
    for step in FAR_FIRST:
        for peer in (y_peer(step), z_peer(step), corner_peer(step)):
            pl.semaphore_signal(barrier, inc=1, device_id=peer, device_id_type=MESH)

    def block_of(px, pz, pcore):
        return column_buf.at[px * 2 + lax.div(pz, 4), lax.rem(pz, 4), pcore]

    own_copies = [
        pltpu.make_async_copy(
            samples.at[pl.ds(64 * piece, 64)],
            row_buf.at[2 * y + piece // 2, piece % 2],
            own_sem.at[piece],
        )
        for piece in range(PIECES)
    ]
    own_copies.append(
        pltpu.make_async_copy(references, block_of(x, z, core), own_sem.at[PIECES])
    )
    for copy in own_copies:
        copy.start()

    pl.semaphore_wait(barrier, 21)

    def gather(source, target, index, device):
        copy = remote(source, target, gather_send.at[*index], gather_recv.at[*index], device)
        copy.start()
        return copy

    z_copies = {
        step: gather(references, block_of(x, z, core), (0, step), z_peer(step))
        for step in (1, 7, 2, 6, 3, 5, 4)
    }
    x_copies = {}

    def forward(step):
        origin = lax.rem(z + (8 - step), 8)
        landing = block_of(x, origin, core)
        for x_step in (2, 1, 3):
            x_copies[x_step, step] = gather(
                references if step == 0 else landing,
                landing,
                (x_step, step),
                at(lax.rem(x + x_step, 4), z, core),
            )

    ring = {}

    def ring_start(hop, turn):
        for side in (0, 1):
            back = hop - 1
            piece = turn if side == 0 else PIECES - 1 - turn
            block = lax.rem(y + (8 - back if side == 0 else back), 8)
            landing = row_buf.at[2 * block + piece // 2, piece % 2]
            source = samples.at[pl.ds(64 * piece, 64)] if hop == 1 else landing
            copy = remote(
                source,
                landing,
                ring_send.at[side, back, turn],
                ring_recv.at[side, back, turn],
                y_peer(1 if side == 0 else 7),
            )
            copy.start()
            ring[side, hop, turn] = copy

    def ring_wait(hop, turn):
        for side in (0, 1):
            ring[side, hop, turn].wait_recv()

    def ring_turn(hop, turn):
        ring_wait(hop, turn)
        if hop < 3 or (hop == 3 and turn < PIECES // 2):
            ring_start(hop + 1, turn)

    for turn in range(PIECES):
        ring_start(1, turn)
    forward(0)

    in_use = counts[0, 0]
    row_place = lax.broadcasted_iota(jnp.int32, (ROW_TILES, TILE), 0)
    column_place = lax.broadcasted_iota(jnp.int32, (COLUMN_TILES, TILE), 0)

    def mark(slot, carry):
        spare = jnp.where(slot < in_use, 0.0, LOWEST).astype(jnp.float32)
        row_bias[slot] = jnp.where(row_place == pairs[0, 0, 0, slot], spare, LOWEST)
        column_bias[slot] = jnp.where(column_place == pairs[0, 0, 1, slot], spare, LOWEST)
        return carry

    lax.fori_loop(0, SLOTS, mark, 0)
    spread(SCALE * start[...], column_spread)

    for turn, steps in enumerate(((1, 7), (2, 6), (3, 5), (4,))):
        for step in steps:
            z_copies[step].wait_recv()
            forward(step)
        ring_turn(1, turn)
    for copy in own_copies:
        copy.wait()

    core_copies = []

    def swap(step):
        group = lax.rem(x + (4 - step), 4)
        mine = column_buf.at[pl.ds(2 * group, 2), :, core]
        core_copies.append(gather(mine, mine, (4, step), at(x, z, 1 - core)))

    def row_tile(tile):
        return row_buf[tile].reshape(TILE, WIDTH)

    def column_tile(tile):
        return column_buf[tile].reshape(TILE, WIDTH)

    def multiply(steps, groups):
        for step in steps:
            first = 2 * lax.rem(y + step, 8)
            row_values = row_buf[pl.ds(first, 2)].reshape(2 * TILE, WIDTH)
            for group in groups:
                pair = lax.rem(x + (4 - group), 4)
                column_values = column_buf[pl.ds(2 * pair, 2)].reshape(2 * TILE, WIDTH)
                by_column = (2.0 * SCALE) * dot_rows(column_values, row_values)
                by_row = (2.0 * SCALE) * dot_rows(row_values, column_values)
                for i in (0, 1):
                    for j in (0, 1):
                        rows = slice(i * TILE, (i + 1) * TILE)
                        columns = slice(j * TILE, (j + 1) * TILE)
                        place = (first + i) * COLUMN_TILES + 2 * pair + j
                        column_major[place] = by_column[columns, rows]
                        row_major[place] = by_row[rows, columns]

    def level(group):
        for half in (0, 1):
            tile = 2 * lax.rem(x + (4 - group), 4) + half
            values = column_tile(tile).astype(jnp.float32)
            norms = jnp.sum(values * values, axis=1, keepdims=True)
            column_spread[tile] = column_spread[tile] - SCALE * norms

    swap(0)
    ring_turn(2, 0)
    core_copies[0].wait_recv()
    multiply((0, 1, 7), (0,))
    level(0)
    ring_turn(2, 1)
    ring_turn(2, 2)
    ring_turn(2, 3)
    for x_step in (1, 3, 2):
        for step in range(8):
            x_copies[x_step, step].wait_recv()
        swap(x_step)
    multiply((2, 6), (0,))
    ring_turn(3, 0)
    core_copies[1].wait_recv()
    multiply((0, 1, 7), (1,))
    level(1)
    ring_turn(3, 1)
    core_copies[2].wait_recv()
    multiply((0, 1, 7), (3,))
    level(3)
    core_copies[3].wait_recv()
    multiply((0, 1, 7), (2,))
    level(2)
    multiply((2, 6), (1, 3, 2))
    ring_turn(3, 2)
    ring_turn(3, 3)
    multiply((3, 5), (0, 1, 2, 3))
    ring_wait(4, 0)
    ring_wait(4, 1)
    multiply((4,), (0, 1, 2, 3))

    def local_pass(products, spread_ref, axis, bias):
        shape = bias.shape[1:]

        def one(slot, highest):
            row_id = pairs[0, 0, 0, slot]
            column_id = pairs[0, 0, 1, slot]
            place = row_id * COLUMN_TILES + column_id
            scores = products[place] + spread_ref[column_id if axis else row_id]
            peak = jnp.max(scores, axis=0, keepdims=True)
            slot_peak[pl.ds(slot, 1), :] = peak
            slot_total[pl.ds(slot, 1), :] = jnp.sum(
                jnp.exp2(scores - peak), axis=0, keepdims=True
            )
            return jnp.maximum(highest, peak + bias[slot])

        peak = lax.fori_loop(
            0, SLOTS, one, jnp.full(shape, LOWEST, jnp.float32), unroll=48
        )

        def collect(slot, total):
            scale = jnp.exp2(slot_peak[pl.ds(slot, 1), :] + bias[slot] - peak)
            return total + slot_total[pl.ds(slot, 1), :] * scale

        total = lax.fori_loop(
            0, SLOTS, collect, jnp.zeros(shape, jnp.float32), unroll=48
        )
        return peak + jnp.log2(total)

    def exchange(value, buf, iteration, place, peer, send_sem, recv_sem):
        buf[iteration, place] = value
        copies = []
        for step in FAR_FIRST:
            mine = buf.at[iteration, place]
            copy = remote(
                mine,
                mine,
                send_sem.at[iteration, step],
                recv_sem.at[iteration, step],
                peer(step),
            )
            copy.start()
            copies.append(copy)
        return copies

    def finish(copies, buf, iteration):
        for copy in copies:
            copy.wait()
        return log_sum(buf[iteration])

    sample_logs = jnp.log2(sample_mass[...])
    reference_logs = jnp.log2(reference_mass[...])
    for iteration in range(ITERS):
        value = local_pass(column_major, column_spread, 1, row_bias)
        copies = exchange(value, y_buf, iteration, y, y_peer, y_send, y_recv)
        if iteration == 0:
            row_norms = tile_norms(row_tile, ROW_TILES)
        row_level = sample_logs - finish(copies, y_buf, iteration)
        spread(row_level, row_spread)
        if iteration == ITERS - 1:
            sample_out[...] = row_level * (1.0 / SCALE) + row_norms
        value = local_pass(row_major, row_spread, 0, column_bias)
        copies = exchange(value, x_buf, iteration, corner, corner_peer, x_send, x_recv)
        value = finish(copies, x_buf, iteration)
        copies = exchange(value, z_buf, iteration, z, z_peer, z_send, z_recv)
        if iteration == 0:
            column_norms = tile_norms(column_tile, COLUMN_TILES)
        column_level = reference_logs - finish(copies, z_buf, iteration)
        if iteration < ITERS - 1:
            spread(column_level, column_spread)
        else:
            reference_out[...] = column_level * (1.0 / SCALE) + column_norms

    for copy in ring.values():
        copy.wait_send()
    for copy in [*z_copies.values(), *x_copies.values(), *core_copies]:
        copy.wait_send()


def deliver(sample_ref, reference_ref, sample_out, reference_out):
    sample_out[...] = sample_ref[...]
    reference_out[...] = reference_ref[...]


def body(
    sample_embeddings,
    reference_embeddings,
    sample_mass,
    reference_mass,
    start_potential,
    tile_pairs,
    tile_counts,
):
    vmem = pl.BlockSpec(memory_space=pltpu.VMEM)
    smem = pl.BlockSpec(memory_space=pltpu.SMEM)
    anywhere = pl.BlockSpec(memory_space=pl.ANY)
    dma = pltpu.SemaphoreType.DMA
    sample_out, reference_out = pl.pallas_call(
        kernel,
        out_shape=(
            jax.ShapeDtypeStruct((ROW_TILES, TILE), jnp.float32),
            jax.ShapeDtypeStruct((COLUMN_TILES, TILE), jnp.float32),
        ),
        in_specs=[anywhere, anywhere, vmem, vmem, vmem, smem, smem],
        out_specs=(vmem, vmem),
        scratch_shapes=[
            pltpu.VMEM((ROW_TILES, 2, 64, WIDTH), jnp.bfloat16),
            pltpu.VMEM((COLUMN_TILES, 4, 2, 16, WIDTH), jnp.bfloat16),
            pltpu.VMEM((ROW_TILES * COLUMN_TILES, TILE, TILE), jnp.float32),
            pltpu.VMEM((ROW_TILES * COLUMN_TILES, TILE, TILE), jnp.float32),
            pltpu.VMEM((COLUMN_TILES, TILE, TILE), jnp.float32),
            pltpu.VMEM((ROW_TILES, TILE, TILE), jnp.float32),
            pltpu.VMEM((SLOTS, TILE), jnp.float32),
            pltpu.VMEM((SLOTS, TILE), jnp.float32),
            pltpu.VMEM((SLOTS, ROW_TILES, TILE), jnp.float32),
            pltpu.VMEM((SLOTS, COLUMN_TILES, TILE), jnp.float32),
            pltpu.VMEM((ITERS, 8, ROW_TILES, TILE), jnp.float32),
            pltpu.VMEM((ITERS, 8, COLUMN_TILES, TILE), jnp.float32),
            pltpu.VMEM((ITERS, 8, COLUMN_TILES, TILE), jnp.float32),
            dma((PIECES + 1,)),
            dma((2, 4, PIECES)),
            dma((2, 4, PIECES)),
            dma((5, 8)),
            dma((5, 8)),
            dma((ITERS, 8)),
            dma((ITERS, 8)),
            dma((ITERS, 8)),
            dma((ITERS, 8)),
            dma((ITERS, 8)),
            dma((ITERS, 8)),
        ],
        compiler_params=pltpu.CompilerParams(collective_id=0, has_side_effects=True),
    )(
        sample_embeddings,
        reference_embeddings,
        sample_mass.reshape(ROW_TILES, TILE),
        reference_mass.reshape(COLUMN_TILES, TILE),
        start_potential.reshape(COLUMN_TILES, TILE),
        tile_pairs,
        tile_counts,
    )
    sample_out, reference_out = pl.pallas_call(
        deliver,
        out_shape=(
            jax.ShapeDtypeStruct((ROW_TILES, TILE), jnp.float32),
            jax.ShapeDtypeStruct((COLUMN_TILES, TILE), jnp.float32),
        ),
        in_specs=[vmem, vmem],
        out_specs=(vmem, vmem),
    )(sample_out, reference_out)
    return (sample_out.reshape(-1), reference_out.reshape(-1))


def solution(mesh):
    placed = (
        P(("rows", "cols"), None),
        P(("cols", "rows"), None),
        P("rows"),
        P("cols"),
        P("cols"),
        P("rows", "cols", None, None),
        P("rows", "cols"),
    )
    return jax.shard_map(
        body, mesh=mesh, in_specs=placed, out_specs=(P("rows"), P("cols")), check_vma=False
    )
```
